128 devices in a mesh: dom: 16 (over x, z), grid: 8 (over y, core).
Axes of the slice: x: 4, y: 4, z: 4, core: 2. Of those that a mesh axis runs over, the one named last changes fastest.
Arguments:
- adjoint: float32 [8, 6, 2048, 128], P('grid', None, 'dom'), may hold values from -6 to 6
- jac_diag: float32 [8, 6, 6, 2048, 128], P('grid', None, None, 'dom'), may hold values from -6 to 6
- jac_face: float32 [8, 6, 4, 6, 2048, 128], P('grid', None, None, None, 'dom'), may hold values from -3 to 3
- metric: float32 [8, 6, 3, 4, 2048, 128], P('grid', None, None, None, 'dom'), may hold values from -1.5 to 1.5
- node_id: int32 [8, 4, 2048, 128], P('grid', None, 'dom'), may hold values from 0 to 65535
- fringe_cell: int32 [128, 128, 128], P(('dom', 'grid')), may hold values from 0 to 16383
- donor_cell: int32 [128, 128, 128], P(('dom', 'grid')), may hold values from 0 to 16383
- fringe_weight: float32 [128, 128, 128], P(('dom', 'grid')), may hold values from 0.05 to 1
- donor_count: int32 [128, 128], P(('dom', 'grid')), may hold values from 16 to 128, as said below
Outputs:
- product: float32 [8, 6, 2048, 128], P('grid', None, 'dom')
- node_sens: float32 [3, 65536], P(None, ('dom', 'grid'))
The draws below stay inside these ranges and needn't reach their ends.
Inputs may be any that keep to these rules, and one draw needn't show every extreme that they name: The live slots from p to q are slots 0 to donor_count[q, p] - 1; in every draw some receiving device has 128 live slots from every sender.
All inputs are finite; a program needn't handle non-finite values.
Results may differ from the reference program's by a relative error of at most 0.000071.
Values sent between devices are 32-bit elements; how exact they have to be, the bound alone decides.
A program may use at most 192 MiB of HBM per device.

```python
import math
import jax
import jax.numpy as jnp
from jax import lax

NVAR = 6
BLOCK = 128
FACES = 4
CORNERS = 4
COORDS = 3
ROWS_DEV = 128
CAP = 128
GRIDS = 8
ROWS = 2048
NODES = 65536
N_DOM = 16
DEVICES = 128


def draw_donor_count(key, part):
    key_counts = jax.random.fold_in(key, 11)
    key_full = jax.random.fold_in(key, 23)
    counts = jax.random.randint(key_counts, (DEVICES, DEVICES), CAP // 8, CAP + 1)
    full_row = jax.random.randint(key_full, (), 0, DEVICES)
    row_ids = jnp.arange(DEVICES)[:, None]
    return jnp.where(row_ids == full_row, CAP, counts).astype(jnp.int32)


def set_ends(result, stream_key, smallest, largest):
    extent = result.shape
    index_at = [jax.random.randint(jax.random.fold_in(stream_key, axis), (), 0, extent[axis]) for axis in range(len(extent))]
    result = result.at[tuple(index_at)].set(smallest)
    longest = extent.index(max(extent))
    index_at[longest] = (index_at[longest] + 1) % extent[longest]
    return result.at[tuple(index_at)].set(largest)


def levels(stream_key, extent, cuts, smallest, largest):
    gain = 1.0
    for position, blocks in cuts:
        draws = jax.random.uniform(jax.random.fold_in(jax.random.fold_in(stream_key, 6), position), (blocks,), jnp.float32, smallest / len(cuts), largest / len(cuts))
        gain = gain * jnp.repeat(jnp.exp(draws), extent[position] // blocks).reshape((-1,) + (1,) * (len(extent) - 1 - position))
    return gain


def scatter_about(key, dims, deviation, most, split=(), kind=jnp.bfloat16):
    level = levels(key, dims, split, -0.22, 0.18) if split else 1.0
    array = jax.random.normal(key, dims, jnp.float32) * deviation * level
    return jnp.minimum(jnp.maximum(array, -most), most).astype(kind)


def setup_inputs(seed: int = 0) -> dict:
    streams_of = jax.random.split(jax.random.key(seed), 10)
    return {
        "adjoint": scatter_about(streams_of[0], (GRIDS, NVAR, ROWS, BLOCK), 1.0, 6.0, ((0, 8), (2, 16)), jnp.float32),
        "jac_diag": scatter_about(streams_of[1], (GRIDS, NVAR, NVAR, ROWS, BLOCK), 0.4, 6.0, ((0, 8), (3, 16)), jnp.float32),
        "jac_face": scatter_about(streams_of[2], (GRIDS, NVAR, FACES, NVAR, ROWS, BLOCK), 0.2, 3.0, ((0, 8), (4, 16)), jnp.float32),
        "metric": scatter_about(streams_of[3], (GRIDS, NVAR, COORDS, CORNERS, ROWS, BLOCK), 0.1, 1.5, ((0, 8), (4, 16)), jnp.float32),
        "node_id": set_ends(jax.random.randint(streams_of[4], (GRIDS, CORNERS, ROWS, BLOCK), 0, NODES), jax.random.fold_in(streams_of[4], 1), 0, NODES - 1).astype(jnp.int32),
        "fringe_cell": set_ends(jax.random.randint(streams_of[5], (DEVICES, DEVICES, CAP), 0, ROWS_DEV * BLOCK), jax.random.fold_in(streams_of[5], 1), 0, (ROWS_DEV * BLOCK) - 1).astype(jnp.int32),
        "donor_cell": set_ends(jax.random.randint(streams_of[6], (DEVICES, DEVICES, CAP), 0, ROWS_DEV * BLOCK), jax.random.fold_in(streams_of[6], 1), 0, (ROWS_DEV * BLOCK) - 1).astype(jnp.int32),
        "fringe_weight": jnp.clip(jnp.exp(math.log(1.0) - 2.9957323 * jax.random.uniform(streams_of[7], (DEVICES, DEVICES, CAP), jnp.float32) ** levels(streams_of[7], (DEVICES, DEVICES, CAP), ((0, 128),), -0.2, 0.2)), 0.05, 1.0),
        "donor_count": draw_donor_count(jax.random.fold_in(streams_of[9], 71), 0),
    }


def to_devices(array_field):
    grid_count, var_count = array_field.shape[0], array_field.shape[1]
    by_owner = array_field.reshape(grid_count, var_count, N_DOM, ROWS_DEV * BLOCK)
    return jnp.transpose(by_owner, (2, 0, 1, 3)).reshape(N_DOM * grid_count, var_count, ROWS_DEV * BLOCK)


def from_devices(stacked):
    var_count = stacked.shape[1]
    by_owner = stacked.reshape(N_DOM, GRIDS, var_count, ROWS_DEV * BLOCK)
    return jnp.transpose(by_owner, (1, 2, 0, 3)).reshape(GRIDS, var_count, ROWS, BLOCK)


def pick_slots(values, cell_ids):
    return jnp.take(values, cell_ids, axis=1)


def deposit(values, cell_ids, weights):
    empty = jnp.zeros((NVAR, ROWS_DEV * BLOCK), jnp.float32)
    return empty.at[:, cell_ids].add(-(values * weights[None]))


def reference(adjoint, jac_diag, jac_face, metric, node_id, fringe_cell, donor_cell, fringe_weight, donor_count):
    highest = lax.Precision.HIGHEST
    diagonal_part = jnp.einsum('gijrc,girc->gjrc', jac_diag, adjoint, precision=highest)
    face_terms = jnp.einsum('gifjrc,girc->gfjrc', jac_face, adjoint, precision=highest)
    carried = jnp.pad(face_terms[:, 0, :, 1:, :], ((0, 0), (0, 0), (0, 1), (0, 0)))
    carried = carried + jnp.pad(face_terms[:, 1, :, :-1, :], ((0, 0), (0, 0), (1, 0), (0, 0)))
    carried = carried + jnp.pad(face_terms[:, 2, :, :, 1:], ((0, 0), (0, 0), (0, 0), (0, 1)))
    carried = carried + jnp.pad(face_terms[:, 3, :, :, :-1], ((0, 0), (0, 0), (0, 0), (1, 0)))
    adjoint_dev = to_devices(adjoint)
    payload = jax.vmap(pick_slots)(adjoint_dev, fringe_cell)
    received = jnp.transpose(payload, (2, 1, 0, 3))
    live_slots = jnp.arange(CAP, dtype=jnp.int32)[None, None, :] < donor_count[:, :, None]
    slot_weights = jnp.where(live_slots, fringe_weight, jnp.zeros_like(fringe_weight))
    interp_dev = jax.vmap(deposit)(received, donor_cell, slot_weights)
    product = diagonal_part + carried + from_devices(interp_dev)
    corner_terms = jnp.einsum('gixkrc,girc->xgkrc', metric, adjoint, precision=highest)
    node_sens = jnp.zeros((COORDS, NODES), jnp.float32).at[:, node_id.reshape(-1)].add(corner_terms.reshape(COORDS, -1))
    return product, node_sens
```

```python
import jax
import jax.numpy as jnp
from jax import lax
from jax.experimental import pallas as pl
from jax.experimental.pallas import tpu as pltpu
from jax.sharding import PartitionSpec as P

BF = jnp.bfloat16
F32 = jnp.float32
VMEM_LIMIT = 60 * 2**20


def spread(row, rows):
    tile = jnp.broadcast_to(row, (16, row.shape[1])).astype(BF)
    return jnp.concatenate([tile] * (rows // 16), axis=0)


def ids(rows):
    return lax.broadcasted_iota(jnp.int32, (rows, 128), 0).astype(F32).astype(BF)


def halves(value):
    high = value.astype(BF).astype(F32)
    return high, value - high


def onehot(mask):
    return jnp.where(mask, jnp.ones((), BF), jnp.zeros((), BF))


def gather_kernel(adj_ref, cell_ref, out_ref, table):
    step = pl.program_id(0)

    @pl.when(step == 0)
    def _():
        for v in range(6):
            high, low = halves(adj_ref[v])
            table[v * 128:(v + 1) * 128, :128] = high.astype(BF)
            table[v * 128:(v + 1) * 128, 128:] = low.astype(BF)

    lane_ids = ids(128)
    row_ids = lax.broadcasted_iota(jnp.int32, (128, 128), 0)
    cells = cell_ref[...]
    rows, lanes = cells >> 7, (cells & 127).astype(F32)
    for pair in range(4):
        js = (2 * pair, 2 * pair + 1)
        pick = jnp.concatenate([onehot(lane_ids == spread(lanes[j:j + 1], 128)) for j in js], 1)
        pick = jnp.concatenate([pick, pick], 0)
        hits = [row_ids == jnp.broadcast_to(rows[j:j + 1], (128, 128)) for j in js]
        for v in range(6):
            found = jnp.dot(table[v * 128:(v + 1) * 128, :], pick, preferred_element_type=F32)
            for side, j in enumerate(js):
                part = jnp.where(hits[side], found[:, side * 128:(side + 1) * 128], 0.0)
                out_ref[j, v:v + 1, :] = jnp.sum(part, axis=0, keepdims=True)


def gather(adj, cells):
    return pl.pallas_call(
        gather_kernel,
        grid=(16,),
        in_specs=[
            pl.BlockSpec((6, 128, 128), lambda s: (0, 0, 0)),
            pl.BlockSpec((8, 128), lambda s: (s, 0)),
        ],
        out_specs=pl.BlockSpec((8, 6, 128), lambda s: (s, 0, 0)),
        out_shape=jax.ShapeDtypeStruct((128, 6, 128), F32),
        scratch_shapes=[pltpu.VMEM((768, 256), BF)],
        compiler_params=pltpu.CompilerParams(vmem_limit_bytes=VMEM_LIMIT),
        cost_estimate=pl.CostEstimate(flops=6 * 10**9, bytes_accessed=10**6, transcendentals=0),
        name="fringe_gather",
    )(adj, cells)


def node_kernel(adj_ref, met_ref, nid_ref, out_ref, acc):
    step = pl.program_id(0)

    @pl.when(step == 0)
    def _():
        acc[...] = jnp.zeros_like(acc)

    row_ids = ids(256)
    zero = jnp.zeros((256, 128), BF)
    depth = 4

    def corner(k, carry):
        n = nid_ref[k]
        high = (((n >> 8) & 1) * 128 + (n >> 9)).astype(F32)
        low = (n & 255).astype(F32)
        terms = []
        for x in range(3):
            term = met_ref[0, x, k] * adj_ref[0]
            for i in range(1, 6):
                term = term + met_ref[i, x, k] * adj_ref[i]
            terms += halves(term)
        for group in range(8 // depth):
            js = range(group * depth, (group + 1) * depth)
            lows = jnp.concatenate([onehot(row_ids == spread(low[j:j + 1], 256)) for j in js], 1)
            masks = [row_ids == spread(high[j:j + 1], 256) for j in js]
            for t in range(6):
                highs = jnp.concatenate(
                    [jnp.where(m, spread(terms[t][j:j + 1], 256), zero) for m, j in zip(masks, js)], 1
                )
                acc[t] += lax.dot_general(
                    highs, lows, (((1,), (1,)), ((), ())), preferred_element_type=F32
                )
        return carry

    lax.fori_loop(0, 4, corner, 0)

    @pl.when(step == pl.num_programs(0) - 1)
    def _():
        out_ref[...] = jnp.zeros_like(out_ref)
        for x in range(3):
            for e in range(2):
                both = acc[2 * x, e * 128:(e + 1) * 128, :] + acc[2 * x + 1, e * 128:(e + 1) * 128, :]
                for b in range(2):
                    out_ref[pl.ds(x * 4 + e * 2 + b, 128, stride=16), :] = both[:, b * 128:(b + 1) * 128]


def node_partial(adj, metric, node_id):
    return pl.pallas_call(
        node_kernel,
        grid=(16,),
        in_specs=[
            pl.BlockSpec((6, 8, 128), lambda s: (0, s, 0)),
            pl.BlockSpec((6, 3, 4, 8, 128), lambda s: (0, 0, 0, s, 0)),
            pl.BlockSpec((4, 8, 128), lambda s: (0, s, 0)),
        ],
        out_specs=pl.BlockSpec((2048, 128), lambda s: (0, 0)),
        out_shape=jax.ShapeDtypeStruct((2048, 128), F32),
        scratch_shapes=[pltpu.VMEM((6, 256, 256), F32)],
        compiler_params=pltpu.CompilerParams(vmem_limit_bytes=VMEM_LIMIT),
        cost_estimate=pl.CostEstimate(flops=52 * 10**9, bytes_accessed=6 * 10**6, transcendentals=0),
        name="node_scatter",
    )(adj, metric, node_id)


def interp_kernel(recv_ref, cell_ref, weight_ref, count_ref, out_ref, acc):
    step = pl.program_id(0)

    @pl.when(step == 0)
    def _():
        acc[...] = jnp.zeros_like(acc)

    ids_low, ids_high = ids(256), ids(64)
    zero = jnp.zeros((64, 128), BF)
    depth = 4

    def senders(block, carry):
        rows8 = pl.ds(block * 8, 8)
        cells = cell_ref[rows8]
        rows, cols = cells >> 7, cells & 127
        high = (rows & 63).astype(F32)
        low = ((rows >> 6) * 128 + cols).astype(F32)
        live = lax.broadcasted_iota(jnp.int32, (8, 128), 1) < count_ref[rows8]
        weights = jnp.where(live, weight_ref[rows8], 0.0)
        values = [halves(-(recv_ref[rows8, i, :] * weights)) for i in range(6)]
        for group in range(8 // depth):
            js = range(group * depth, (group + 1) * depth)
            lows = jnp.concatenate([onehot(ids_low == spread(low[j:j + 1], 256)) for j in js], 1)
            masks = [ids_high == spread(high[j:j + 1], 64) for j in js]
            for third in range(3):
                highs = jnp.concatenate(
                    [
                        jnp.concatenate(
                            [jnp.where(m, spread(values[i][part][j:j + 1], 64), zero) for m, j in zip(masks, js)], 1
                        )
                        for i in (2 * third, 2 * third + 1)
                        for part in range(2)
                    ],
                    0,
                )
                acc[third] += lax.dot_general(
                    highs, lows, (((1,), (1,)), ((), ())), preferred_element_type=F32
                )
        return carry

    lax.fori_loop(0, 4, senders, 0)

    @pl.when(step == pl.num_programs(0) - 1)
    def _():
        for i in range(6):
            start = (i % 2) * 128
            both = acc[i // 2, start:start + 64, :] + acc[i // 2, start + 64:start + 128, :]
            out_ref[i, :64, :] = both[:, :128]
            out_ref[i, 64:, :] = both[:, 128:]


def interpolate(received, cells, weights, counts):
    return pl.pallas_call(
        interp_kernel,
        grid=(4,),
        in_specs=[
            pl.BlockSpec((32, 6, 128), lambda s: (s, 0, 0)),
            pl.BlockSpec((32, 128), lambda s: (s, 0)),
            pl.BlockSpec((32, 128), lambda s: (s, 0)),
            pl.BlockSpec((32, 1), lambda s: (s, 0)),
        ],
        out_specs=pl.BlockSpec((6, 128, 128), lambda s: (0, 0, 0)),
        out_shape=jax.ShapeDtypeStruct((6, 128, 128), F32),
        scratch_shapes=[pltpu.VMEM((3, 256, 256), F32)],
        compiler_params=pltpu.CompilerParams(vmem_limit_bytes=VMEM_LIMIT),
        cost_estimate=pl.CostEstimate(flops=6 * 10**9, bytes_accessed=10**6, transcendentals=0),
        name="donor_scatter",
    )(received, cells, weights, counts)


def shifted(block, axis, distance):
    devices = range(lax.axis_size(axis))
    route = [(i - distance, i) for i in devices if i - distance in devices]
    return lax.ppermute(block, axis, route)


def contract(blocks, adjoint_local):
    running = blocks[0] * adjoint_local[0]
    for variable in range(1, adjoint_local.shape[0]):
        running = running + blocks[variable] * adjoint_local[variable]
    return running


def local(
    adjoint,
    jac_diag,
    jac_face,
    metric,
    node_id,
    fringe_cell,
    donor_cell,
    fringe_weight,
    donor_count,
):
    values = adjoint[0]
    row_count = values.shape[1]
    payload = gather(values, fringe_cell[0])
    received = lax.all_to_all(payload, ("dom", "grid"), split_axis=0, concat_axis=0, tiled=True)
    partial_value = node_partial(values, metric[0], node_id[0])
    owned = lax.psum_scatter(partial_value, ("dom", "grid"), scatter_dimension=0, tiled=True)
    node_sens = owned[:12].reshape(3, 512)

    diagonal_part = contract(jac_diag[0], values)
    face_terms = contract(jac_face[0], values)
    from_below = shifted(face_terms[0, :, 0, :], "dom", -1)
    from_above = shifted(face_terms[1, :, row_count - 1, :], "dom", 1)
    carried = jnp.concatenate([face_terms[0, :, 1:, :], from_below[:, None, :]], axis=1)
    carried = carried + jnp.concatenate([from_above[:, None, :], face_terms[1, :, :-1, :]], axis=1)
    carried = carried + jnp.pad(face_terms[2, :, :, 1:], ((0, 0), (0, 0), (0, 1)))
    carried = carried + jnp.pad(face_terms[3, :, :, :-1], ((0, 0), (0, 0), (1, 0)))
    interp = interpolate(received, donor_cell[0], fringe_weight[0], donor_count.reshape(128, 1))
    product = diagonal_part + carried + interp
    return (product[None], node_sens)


def solution(mesh):
    in_specs = (
        P("grid", None, "dom", None),
        P("grid", None, None, "dom", None),
        P("grid", None, None, None, "dom", None),
        P("grid", None, None, None, "dom", None),
        P("grid", None, "dom", None),
        P(("dom", "grid"), None, None),
        P(("dom", "grid"), None, None),
        P(("dom", "grid"), None, None),
        P(("dom", "grid"), None),
    )
    out_specs = (P("grid", None, "dom", None), P(None, ("dom", "grid")))
    return jax.shard_map(local, mesh=mesh, in_specs=in_specs, out_specs=out_specs, check_vma=False)
```

```python
import jax
import jax.numpy as jnp
from jax import lax
from jax.experimental import pallas as pl
from jax.experimental.pallas import tpu as pltpu
from jax.sharding import PartitionSpec as P

BF = jnp.bfloat16
F32 = jnp.float32
VMEM_LIMIT = 60 * 2**20


def spread(row, rows):
    tile = jnp.broadcast_to(row, (16, row.shape[1])).astype(BF)
    return jnp.concatenate([tile] * (rows // 16), axis=0)


def ids(rows):
    return lax.broadcasted_iota(jnp.int32, (rows, 128), 0).astype(F32).astype(BF)


def halves(value):
    high = value.astype(BF).astype(F32)
    return high, value - high


def onehot(mask):
    return jnp.where(mask, jnp.ones((), BF), jnp.zeros((), BF))


def gather_kernel(adj_ref, cell_ref, out_ref, table):
    step = pl.program_id(0)

    @pl.when(step == 0)
    def _():
        for v in range(6):
            high, low = halves(adj_ref[v])
            table[v * 128:(v + 1) * 128, :128] = high.astype(BF)
            table[v * 128:(v + 1) * 128, 128:] = low.astype(BF)

    lane_ids = ids(128)
    row_ids = lax.broadcasted_iota(jnp.int32, (128, 128), 0)
    cells = cell_ref[...]
    rows, lanes = cells >> 7, (cells & 127).astype(F32)
    for pair in range(4):
        js = (2 * pair, 2 * pair + 1)
        pick = jnp.concatenate([onehot(lane_ids == spread(lanes[j:j + 1], 128)) for j in js], 1)
        pick = jnp.concatenate([pick, pick], 0)
        hits = [row_ids == jnp.broadcast_to(rows[j:j + 1], (128, 128)) for j in js]
        for v in range(6):
            found = jnp.dot(table[v * 128:(v + 1) * 128, :], pick, preferred_element_type=F32)
            for side, j in enumerate(js):
                part = jnp.where(hits[side], found[:, side * 128:(side + 1) * 128], 0.0)
                out_ref[j, v:v + 1, :] = jnp.sum(part, axis=0, keepdims=True)


def gather(adj, cells):
    return pl.pallas_call(
        gather_kernel,
        grid=(16,),
        in_specs=[
            pl.BlockSpec((6, 128, 128), lambda s: (0, 0, 0)),
            pl.BlockSpec((8, 128), lambda s: (s, 0)),
        ],
        out_specs=pl.BlockSpec((8, 6, 128), lambda s: (s, 0, 0)),
        out_shape=jax.ShapeDtypeStruct((128, 6, 128), F32),
        scratch_shapes=[pltpu.VMEM((768, 256), BF)],
        compiler_params=pltpu.CompilerParams(vmem_limit_bytes=VMEM_LIMIT),
        cost_estimate=pl.CostEstimate(flops=6 * 10**9, bytes_accessed=10**6, transcendentals=0),
        name="fringe_gather",
    )(adj, cells)


def node_kernel(adj_ref, met_ref, nid_ref, out_ref, acc):
    step = pl.program_id(0)

    @pl.when(step == 0)
    def _():
        acc[...] = jnp.zeros_like(acc)

    row_ids = ids(256)
    zero = jnp.zeros((256, 128), BF)
    depth = 4

    def corner(k, carry):
        n = nid_ref[k]
        high = (((n >> 8) & 1) * 128 + (n >> 9)).astype(F32)
        low = (n & 255).astype(F32)
        terms = []
        for x in range(3):
            term = met_ref[0, x, k] * adj_ref[0]
            for i in range(1, 6):
                term = term + met_ref[i, x, k] * adj_ref[i]
            terms += halves(term)
        for group in range(8 // depth):
            js = range(group * depth, (group + 1) * depth)
            lows = jnp.concatenate([onehot(row_ids == spread(low[j:j + 1], 256)) for j in js], 1)
            masks = [row_ids == spread(high[j:j + 1], 256) for j in js]
            for t in range(6):
                highs = jnp.concatenate(
                    [jnp.where(m, spread(terms[t][j:j + 1], 256), zero) for m, j in zip(masks, js)], 1
                )
                acc[t] += lax.dot_general(
                    highs, lows, (((1,), (1,)), ((), ())), preferred_element_type=F32
                )
        return carry

    lax.fori_loop(0, 4, corner, 0)

    @pl.when(step == pl.num_programs(0) - 1)
    def _():
        out_ref[...] = jnp.zeros_like(out_ref)
        for x in range(3):
            for e in range(2):
                both = acc[2 * x, e * 128:(e + 1) * 128, :] + acc[2 * x + 1, e * 128:(e + 1) * 128, :]
                for b in range(2):
                    out_ref[pl.ds(x * 4 + e * 2 + b, 128, stride=16), :] = both[:, b * 128:(b + 1) * 128]


def node_partial(adj, metric, node_id):
    return pl.pallas_call(
        node_kernel,
        grid=(16,),
        in_specs=[
            pl.BlockSpec((6, 8, 128), lambda s: (0, s, 0)),
            pl.BlockSpec((6, 3, 4, 8, 128), lambda s: (0, 0, 0, s, 0)),
            pl.BlockSpec((4, 8, 128), lambda s: (0, s, 0)),
        ],
        out_specs=pl.BlockSpec((2048, 128), lambda s: (0, 0)),
        out_shape=jax.ShapeDtypeStruct((2048, 128), F32),
        scratch_shapes=[pltpu.VMEM((6, 256, 256), F32)],
        compiler_params=pltpu.CompilerParams(vmem_limit_bytes=VMEM_LIMIT),
        cost_estimate=pl.CostEstimate(flops=52 * 10**9, bytes_accessed=6 * 10**6, transcendentals=0),
        name="node_scatter",
    )(adj, metric, node_id)


def interp_kernel(recv_ref, cell_ref, weight_ref, count_ref, out_ref, acc):
    step = pl.program_id(0)

    @pl.when(step == 0)
    def _():
        acc[...] = jnp.zeros_like(acc)

    ids_low, ids_high = ids(256), ids(64)
    zero = jnp.zeros((64, 128), BF)
    depth = 4

    def senders(block, carry):
        rows8 = pl.ds(block * 8, 8)
        cells = cell_ref[rows8]
        rows, cols = cells >> 7, cells & 127
        high = (rows & 63).astype(F32)
        low = ((rows >> 6) * 128 + cols).astype(F32)
        live = lax.broadcasted_iota(jnp.int32, (8, 128), 1) < count_ref[rows8]
        weights = jnp.where(live, weight_ref[rows8], 0.0)
        values = [halves(-(recv_ref[rows8, i, :] * weights)) for i in range(6)]
        for group in range(8 // depth):
            js = range(group * depth, (group + 1) * depth)
            lows = jnp.concatenate([onehot(ids_low == spread(low[j:j + 1], 256)) for j in js], 1)
            masks = [ids_high == spread(high[j:j + 1], 64) for j in js]
            for third in range(3):
                highs = jnp.concatenate(
                    [
                        jnp.concatenate(
                            [jnp.where(m, spread(values[i][part][j:j + 1], 64), zero) for m, j in zip(masks, js)], 1
                        )
                        for i in (2 * third, 2 * third + 1)
                        for part in range(2)
                    ],
                    0,
                )
                acc[third] += lax.dot_general(
                    highs, lows, (((1,), (1,)), ((), ())), preferred_element_type=F32
                )
        return carry

    lax.fori_loop(0, 4, senders, 0)

    @pl.when(step == pl.num_programs(0) - 1)
    def _():
        for i in range(6):
            start = (i % 2) * 128
            both = acc[i // 2, start:start + 64, :] + acc[i // 2, start + 64:start + 128, :]
            out_ref[i, :64, :] = both[:, :128]
            out_ref[i, 64:, :] = both[:, 128:]


def interpolate(received, cells, weights, counts):
    return pl.pallas_call(
        interp_kernel,
        grid=(4,),
        in_specs=[
            pl.BlockSpec((32, 6, 128), lambda s: (s, 0, 0)),
            pl.BlockSpec((32, 128), lambda s: (s, 0)),
            pl.BlockSpec((32, 128), lambda s: (s, 0)),
            pl.BlockSpec((32, 1), lambda s: (s, 0)),
        ],
        out_specs=pl.BlockSpec((6, 128, 128), lambda s: (0, 0, 0)),
        out_shape=jax.ShapeDtypeStruct((6, 128, 128), F32),
        scratch_shapes=[pltpu.VMEM((3, 256, 256), F32)],
        compiler_params=pltpu.CompilerParams(vmem_limit_bytes=VMEM_LIMIT),
        cost_estimate=pl.CostEstimate(flops=6 * 10**9, bytes_accessed=10**6, transcendentals=0),
        name="donor_scatter",
    )(received, cells, weights, counts)


def shifted(block, axis, distance):
    devices = range(lax.axis_size(axis))
    route = [(i - distance, i) for i in devices if i - distance in devices]
    return lax.ppermute(block, axis, route)


def contract(blocks, adjoint_local):
    running = blocks[0] * adjoint_local[0]
    for variable in range(1, adjoint_local.shape[0]):
        running = running + blocks[variable] * adjoint_local[variable]
    return running


def local(
    adjoint,
    jac_diag,
    jac_face,
    metric,
    node_id,
    fringe_cell,
    donor_cell,
    fringe_weight,
    donor_count,
):
    values = adjoint[0]
    row_count = values.shape[1]
    payload = gather(values, fringe_cell[0])
    received = lax.all_to_all(payload, ("dom", "grid"), split_axis=0, concat_axis=0, tiled=True)
    partial_value = node_partial(values, metric[0], node_id[0])
    parts = lax.all_to_all(partial_value, ("dom", "grid"), split_axis=0, concat_axis=0, tiled=True)
    node_sens = jnp.sum(parts.reshape(128, 16, 128), axis=0)[:12].reshape(3, 512)

    diagonal_part = contract(jac_diag[0], values)
    face_terms = contract(jac_face[0], values)
    from_below = shifted(face_terms[0, :, 0, :], "dom", -1)
    from_above = shifted(face_terms[1, :, row_count - 1, :], "dom", 1)
    carried = jnp.concatenate([face_terms[0, :, 1:, :], from_below[:, None, :]], axis=1)
    carried = carried + jnp.concatenate([from_above[:, None, :], face_terms[1, :, :-1, :]], axis=1)
    carried = carried + jnp.pad(face_terms[2, :, :, 1:], ((0, 0), (0, 0), (0, 1)))
    carried = carried + jnp.pad(face_terms[3, :, :, :-1], ((0, 0), (0, 0), (1, 0)))
    interp = interpolate(received, donor_cell[0], fringe_weight[0], donor_count.reshape(128, 1))
    product = diagonal_part + carried + interp
    return (product[None], node_sens)


def solution(mesh):
    in_specs = (
        P("grid", None, "dom", None),
        P("grid", None, None, "dom", None),
        P("grid", None, None, None, "dom", None),
        P("grid", None, None, None, "dom", None),
        P("grid", None, "dom", None),
        P(("dom", "grid"), None, None),
        P(("dom", "grid"), None, None),
        P(("dom", "grid"), None, None),
        P(("dom", "grid"), None),
    )
    out_specs = (P("grid", None, "dom", None), P(None, ("dom", "grid")))
    return jax.shard_map(local, mesh=mesh, in_specs=in_specs, out_specs=out_specs, check_vma=False)
```

```python
import jax
import jax.numpy as jnp
from jax import lax
from jax.experimental import pallas as pl
from jax.experimental.pallas import tpu as pltpu
from jax.sharding import PartitionSpec as P

BF = jnp.bfloat16
F32 = jnp.float32
DEVICES = 128
GRIDS = 8
DOMS = 16
MESH = pl.DeviceIdType.MESH


def spread(row, rows):
    tile = jnp.broadcast_to(row, (16, row.shape[1])).astype(BF)
    return jnp.concatenate([tile] * (rows // 16), axis=0)


def ids(rows):
    return lax.broadcasted_iota(jnp.int32, (rows, 128), 0).astype(F32).astype(BF)


def halves(value):
    high = value.astype(BF).astype(F32)
    return high, value - high


def onehot(mask):
    return jnp.where(mask, jnp.ones((), BF), jnp.zeros((), BF))


def place(device):
    return (device // GRIDS, device % GRIDS)


def wait_for(view, semaphore):
    pltpu.make_async_copy(view, view, semaphore).wait()


def send_all(me, source, target, rows, send_sem, recv_sem):
    def one(step, carry):
        q = lax.rem(me + step, DEVICES)
        pltpu.make_async_remote_copy(
            src_ref=source.at[q, pl.ds(0, rows)],
            dst_ref=target.at[me, pl.ds(0, rows)],
            send_sem=send_sem,
            recv_sem=recv_sem,
            device_id=place(q),
            device_id_type=MESH,
        ).start()
        return carry

    lax.fori_loop(1, DEVICES, one, 0)
    pltpu.make_async_copy(source.at[me, pl.ds(0, rows)], target.at[me, pl.ds(0, rows)], recv_sem).start()


def kernel(
    adj, cell, nid, donor, weight, count, diag_hbm, face_hbm, met_hbm,
    product, sens,
    diag, face, met, table, counts, acc,
    pay, recv, part01, got01, part2, got2, halo_out, halo_in,
    local_sem, send_sem, recv_sem, halo_send, halo_recv,
):
    dom, grid = lax.axis_index("dom"), lax.axis_index("grid")
    me = dom * GRIDS + grid
    load_face = pltpu.make_async_copy(face_hbm, face, local_sem.at[0])
    load_met = pltpu.make_async_copy(met_hbm, met, local_sem.at[1])
    load_diag = pltpu.make_async_copy(diag_hbm, diag, local_sem.at[2])
    load_face.start()
    load_met.start()
    load_diag.start()
    barrier = pltpu.get_barrier_semaphore()

    def greet(step, carry):
        q = lax.rem(me + step, DEVICES)
        pl.semaphore_signal(barrier, inc=1, device_id=place(q), device_id_type=MESH)
        return carry

    lax.fori_loop(1, DEVICES, greet, 0)

    for v in range(6):
        high, low = halves(adj[v])
        table[v * 128:(v + 1) * 128, :128] = high.astype(BF)
        table[v * 128:(v + 1) * 128, 128:] = low.astype(BF)
    counts[...] = jnp.broadcast_to(count[...].astype(F32), (128, 128)).T
    ids64, ids128, ids256 = ids(64), ids(128), ids(256)
    row_ids = lax.broadcasted_iota(jnp.int32, (128, 128), 0)
    lane_ids = lax.broadcasted_iota(jnp.int32, (128, 128), 1)

    def fringe(block, carry):
        cells = cell[pl.ds(block * 8, 8), :]
        rows, lanes = cells >> 7, (cells & 127).astype(F32)
        for pair in range(4):
            js = (2 * pair, 2 * pair + 1)
            pick = jnp.concatenate([onehot(ids128 == spread(lanes[j:j + 1], 128)) for j in js], 1)
            pick = jnp.concatenate([pick, pick], 0)
            hits = [row_ids == jnp.broadcast_to(rows[j:j + 1], (128, 128)) for j in js]
            for v in range(6):
                found = jnp.dot(table[v * 128:(v + 1) * 128, :], pick, preferred_element_type=F32)
                for side, j in enumerate(js):
                    mine = jnp.where(hits[side], found[:, side * 128:(side + 1) * 128], 0.0)
                    pay[block * 8 + j, v:v + 1, :] = jnp.sum(mine, axis=0, keepdims=True)
        return carry

    lax.fori_loop(0, 16, fringe, 0)

    load_face.wait()
    for side, row in ((0, 0), (1, 127)):
        edge = face[0, side, :, row, :] * adj[0, row:row + 1, :]
        for i in range(1, 6):
            edge = edge + face[i, side, :, row, :] * adj[i, row:row + 1, :]
        halo_out[side, 0:6, :] = edge

    pl.semaphore_wait(barrier, DEVICES - 1)
    send_all(me, pay, recv, 8, send_sem.at[0], recv_sem.at[0])
    halos = []
    for side, to in ((0, lax.rem(dom + DOMS - 1, DOMS)), (1, lax.rem(dom + 1, DOMS))):
        copy = pltpu.make_async_remote_copy(
            src_ref=halo_out.at[side],
            dst_ref=halo_in.at[side],
            send_sem=halo_send.at[side],
            recv_sem=halo_recv.at[side],
            device_id=(to, grid),
            device_id_type=MESH,
        )
        copy.start()
        halos.append(copy)

    load_met.wait()
    depth = 4
    zero256 = jnp.zeros((256, 128), BF)
    zero64 = jnp.zeros((64, 128), BF)

    def node_pass(xs):
        for t in range(2 * len(xs)):
            acc[t] = jnp.zeros((256, 256), F32)

        def tile(step, carry):
            k, rows8 = step // 16, pl.ds((step % 16) * 8, 8)
            n = nid[k, rows8, :]
            high = (((n >> 8) & 1) * 128 + (n >> 9)).astype(F32)
            low = (n & 255).astype(F32)
            terms = []
            for x in xs:
                term = met[0, x, k, rows8, :] * adj[0, rows8, :]
                for i in range(1, 6):
                    term = term + met[i, x, k, rows8, :] * adj[i, rows8, :]
                terms += halves(term)
            for group in range(8 // depth):
                js = range(group * depth, (group + 1) * depth)
                lows = jnp.concatenate([onehot(ids256 == spread(low[j:j + 1], 256)) for j in js], 1)
                masks = [ids256 == spread(high[j:j + 1], 256) for j in js]
                for t in range(2 * len(xs)):
                    highs = jnp.concatenate(
                        [jnp.where(m, spread(terms[t][j:j + 1], 256), zero256) for m, j in zip(masks, js)], 1
                    )
                    acc[t] += lax.dot_general(
                        highs, lows, (((1,), (1,)), ((), ())), preferred_element_type=F32
                    )
            return carry

        lax.fori_loop(0, 64, tile, 0)

    def node_store(where, slots):
        for slot in range(slots):
            for e in range(2):
                rows = slice(e * 128, (e + 1) * 128)
                both = acc[2 * slot, rows, :] + acc[2 * slot + 1, rows, :]
                for b in range(2):
                    where[:, slot * 4 + e * 2 + b, :] = both[:, b * 128:(b + 1) * 128]

    node_pass((0, 1))
    node_store(part01, 2)
    send_all(me, part01, got01, 8, send_sem.at[1], recv_sem.at[1])
    node_pass((2,))
    node_store(part2, 1)
    send_all(me, part2, got2, 4, send_sem.at[2], recv_sem.at[2])

    wait_for(recv, recv_sem.at[0])
    for t in range(3):
        acc[t] = jnp.zeros((256, 256), F32)

    def senders(block, carry):
        rows8 = pl.ds(block * 8, 8)
        cells = donor[rows8, :]
        rows, cols = cells >> 7, cells & 127
        high = (rows & 63).astype(F32)
        low = ((rows >> 6) * 128 + cols).astype(F32)
        live = lane_ids[0:8].astype(F32) < counts[rows8, :]
        weights = jnp.where(live, weight[rows8, :], 0.0)
        values = [halves(-(recv[rows8, i, :] * weights)) for i in range(6)]
        for group in range(8 // depth):
            js = range(group * depth, (group + 1) * depth)
            lows = jnp.concatenate([onehot(ids256 == spread(low[j:j + 1], 256)) for j in js], 1)
            masks = [ids64 == spread(high[j:j + 1], 64) for j in js]
            for third in range(3):
                highs = jnp.concatenate(
                    [
                        jnp.concatenate(
                            [jnp.where(m, spread(values[i][half][j:j + 1], 64), zero64) for m, j in zip(masks, js)],
                            1,
                        )
                        for i in (2 * third, 2 * third + 1)
                        for half in range(2)
                    ],
                    0,
                )
                acc[third] += lax.dot_general(
                    highs, lows, (((1,), (1,)), ((), ())), preferred_element_type=F32
                )
        return carry

    lax.fori_loop(0, 16, senders, 0)
    for i in range(6):
        start = (i % 2) * 128
        both = acc[i // 2, start:start + 64, :] + acc[i // 2, start + 64:start + 128, :]
        product[i, :64, :] = both[:, :128]
        product[i, 64:, :] = both[:, 128:]

    load_diag.wait()
    for copy in halos:
        copy.wait()
    first, last = row_ids == 0, row_ids == 127
    left, right = lane_ids == 0, lane_ids == 127

    def variable(j, carry):
        def against(block):
            total = block(0) * adj[0]
            for i in range(1, 6):
                total = total + block(i) * adj[i]
            return total

        below = jnp.where(dom == DOMS - 1, 0.0, halo_in[0, pl.ds(j, 1), :])
        above = jnp.where(dom == 0, 0.0, halo_in[1, pl.ds(j, 1), :])
        total = product[j] + against(lambda i: diag[i, j])
        up = pltpu.roll(against(lambda i: face[i, 0, j]), 127, 0)
        total = total + jnp.where(last, jnp.broadcast_to(below, (128, 128)), up)
        down = pltpu.roll(against(lambda i: face[i, 1, j]), 1, 0)
        total = total + jnp.where(first, jnp.broadcast_to(above, (128, 128)), down)
        total = total + jnp.where(right, 0.0, pltpu.roll(against(lambda i: face[i, 2, j]), 127, 1))
        total = total + jnp.where(left, 0.0, pltpu.roll(against(lambda i: face[i, 3, j]), 1, 1))
        product[j] = total
        return carry

    lax.fori_loop(0, 6, variable, 0)

    wait_for(got01, recv_sem.at[1])
    owned = jnp.sum(got01[...], axis=0)
    for x in range(2):
        for b in range(4):
            sens[x:x + 1, b * 128:(b + 1) * 128] = owned[x * 4 + b:x * 4 + b + 1, :]
    wait_for(got2.at[:, pl.ds(0, 4)], recv_sem.at[2])
    owned = jnp.sum(got2[:, 0:4, :], axis=0)
    for b in range(4):
        sens[2:3, b * 128:(b + 1) * 128] = owned[b:b + 1, :]

    others = DEVICES - 1
    wait_for(pay.at[pl.ds(0, others)], send_sem.at[0])
    wait_for(part01.at[pl.ds(0, others)], send_sem.at[1])
    wait_for(part2.at[pl.ds(0, others), pl.ds(0, 4)], send_sem.at[2])


def local(
    adjoint, jac_diag, jac_face, metric, node_id, fringe_cell, donor_cell, fringe_weight, donor_count
):
    vmem = pl.BlockSpec(memory_space=pltpu.VMEM)
    hbm = pl.BlockSpec(memory_space=pl.ANY)
    blocks = pltpu.VMEM((DEVICES, 8, 128), F32)
    product, sens = pl.pallas_call(
        kernel,
        in_specs=[vmem] * 6 + [hbm] * 3,
        out_specs=[vmem, vmem],
        out_shape=[
            jax.ShapeDtypeStruct((6, 128, 128), F32),
            jax.ShapeDtypeStruct((3, 512), F32),
        ],
        scratch_shapes=[
            pltpu.VMEM((6, 6, 128, 128), F32),
            pltpu.VMEM((6, 4, 6, 128, 128), F32),
            pltpu.VMEM((6, 3, 4, 128, 128), F32),
            pltpu.VMEM((768, 256), BF),
            pltpu.VMEM((128, 128), F32),
            pltpu.VMEM((4, 256, 256), F32),
            blocks, blocks, blocks, blocks, blocks, blocks,
            pltpu.VMEM((2, 8, 128), F32),
            pltpu.VMEM((2, 8, 128), F32),
            pltpu.SemaphoreType.DMA((3,)),
            pltpu.SemaphoreType.DMA((3,)),
            pltpu.SemaphoreType.DMA((3,)),
            pltpu.SemaphoreType.DMA((2,)),
            pltpu.SemaphoreType.DMA((2,)),
        ],
        compiler_params=pltpu.CompilerParams(
            collective_id=0, has_side_effects=True, vmem_limit_bytes=58 * 2**20
        ),
        name="adjoint_step",
    )(
        adjoint[0], fringe_cell[0], node_id[0], donor_cell[0], fringe_weight[0], donor_count,
        jac_diag[0], jac_face[0], metric[0],
    )
    return (product[None], sens)


def solution(mesh):
    in_specs = (
        P("grid", None, "dom", None),
        P("grid", None, None, "dom", None),
        P("grid", None, None, None, "dom", None),
        P("grid", None, None, None, "dom", None),
        P("grid", None, "dom", None),
        P(("dom", "grid"), None, None),
        P(("dom", "grid"), None, None),
        P(("dom", "grid"), None, None),
        P(("dom", "grid"), None),
    )
    out_specs = (P("grid", None, "dom", None), P(None, ("dom", "grid")))
    return jax.shard_map(local, mesh=mesh, in_specs=in_specs, out_specs=out_specs, check_vma=False)
```

```python
import jax
import jax.numpy as jnp
from jax import lax
from jax.experimental import pallas as pl
from jax.experimental.pallas import tpu as pltpu
from jax.sharding import PartitionSpec as P

BF = jnp.bfloat16
F8 = jnp.float8_e4m3fn
F32 = jnp.float32
DEVICES = 128
GRIDS = 8
DOMS = 16
MESH = pl.DeviceIdType.MESH


def spread(row, rows):
    tile = jnp.broadcast_to(row, (16, row.shape[1])).astype(BF)
    return jnp.concatenate([tile] * (rows // 16), axis=0)


def spread8(row, kind):
    tile = jnp.broadcast_to(row, (32, row.shape[1])).astype(kind)
    return jnp.concatenate([tile] * 8, axis=0)


def digits(value):
    first = value.astype(F8).astype(F32)
    rest = (value - first) * 16.0
    second = rest.astype(F8).astype(F32)
    return first, second, (rest - second) * 16.0


def ids(rows):
    return lax.broadcasted_iota(jnp.int32, (rows, 128), 0).astype(F32).astype(BF)


def halves(value):
    high = value.astype(BF).astype(F32)
    return high, value - high


def onehot(mask):
    return jnp.where(mask, jnp.ones((), BF), jnp.zeros((), BF))


def partner(me, step):
    device = me + jnp.where(step == DEVICES, DEVICES // 2, step)
    device = jnp.where(device >= DEVICES, device - DEVICES, device)
    return device, (lax.div(device, GRIDS), lax.rem(device, GRIDS))


def wait_for(view, semaphore):
    pltpu.make_async_copy(view, view, semaphore).wait()


class Exchange:
    def __init__(self, me, source, target, rows, send_sem, recv_sem):
        self.me, self.source, self.target, self.rows = me, source, target, rows
        self.send_sem, self.recv_sem = send_sem, recv_sem

    def block(self, ref, index):
        return ref.at[index] if self.rows == 8 else ref.at[index, pl.ds(0, self.rows)]

    def keep(self):
        pltpu.make_async_copy(
            self.block(self.source, self.me), self.block(self.target, self.me), self.recv_sem
        ).start()

    def send(self, step):
        device, coordinates = partner(self.me, step)
        pltpu.make_async_remote_copy(
            src_ref=self.block(self.source, device),
            dst_ref=self.block(self.target, jnp.where(step == DEVICES, DEVICES, self.me)),
            send_sem=self.send_sem,
            recv_sem=self.recv_sem,
            device_id=coordinates,
            device_id_type=MESH,
        ).start()

    def wait_recv(self):
        wait_for(self.block(self.target, pl.ds(0, DEVICES + 1)), self.recv_sem)

    def wait_send(self):
        wait_for(self.block(self.source, pl.ds(0, DEVICES)), self.send_sem)


def kernel(
    adj, cell, nid, donor, weight, count, diag_hbm, face_hbm, met_hbm,
    product, sens,
    diag, face, met, table, counts, acc,
    pay, recv, part01, got01, part2, got2, halo_out, halo_in,
    local_sem, send_sem, recv_sem, halo_send, halo_recv,
):
    dom, grid = lax.axis_index("dom"), lax.axis_index("grid")
    me = dom * GRIDS + grid
    load_face = pltpu.make_async_copy(face_hbm, face, local_sem.at[0])
    load_met = pltpu.make_async_copy(met_hbm, met, local_sem.at[1])
    load_diag = pltpu.make_async_copy(diag_hbm, diag, local_sem.at[2])
    load_face.start()
    load_met.start()
    load_diag.start()
    barrier = pltpu.get_barrier_semaphore()

    for v in range(6):
        high, low = halves(adj[v])
        table[v * 128:(v + 1) * 128, :128] = high.astype(BF)
        table[v * 128:(v + 1) * 128, 128:] = low.astype(BF)
    counts[...] = jnp.broadcast_to(count[...].astype(F32), (128, 128)).T
    ids64, ids128, ids256 = ids(64), ids(128), ids(256)
    row_ids = lax.broadcasted_iota(jnp.int32, (128, 128), 0)
    lane_ids = lax.broadcasted_iota(jnp.int32, (128, 128), 1)

    def fringe(block, carry):
        cells = cell[pl.ds(block * 8, 8), :]
        rows, lanes = cells >> 7, (cells & 127).astype(F32)
        for k in range(8):
            pl.semaphore_signal(
                barrier, inc=1, device_id=partner(me, block * 8 + k + 1)[1], device_id_type=MESH
            )
        for pair in range(4):
            js = (2 * pair, 2 * pair + 1)
            pick = jnp.concatenate([onehot(ids128 == spread(lanes[j:j + 1], 128)) for j in js], 1)
            pick = jnp.concatenate([pick, pick], 0)
            hits = [row_ids == jnp.broadcast_to(rows[j:j + 1], (128, 128)) for j in js]
            found = jnp.dot(table[...], pick, preferred_element_type=F32)
            for v in range(6):
                for side, j in enumerate(js):
                    mine = found[v * 128:(v + 1) * 128, side * 128:(side + 1) * 128]
                    mine = jnp.where(hits[side], mine, 0.0)
                    pay[block * 8 + j, v:v + 1, :] = jnp.sum(mine, axis=0, keepdims=True)
        return carry

    lax.fori_loop(0, 16, fringe, 0)

    load_face.wait()
    for side, row in ((0, 0), (1, 127)):
        edge = face[0, side, :, row, :] * adj[0, row:row + 1, :]
        for i in range(1, 6):
            edge = edge + face[i, side, :, row, :] * adj[i, row:row + 1, :]
        halo_out[side, 0:6, :] = edge

    pl.semaphore_wait(barrier, DEVICES)
    fringes = Exchange(me, pay, recv, 8, send_sem.at[0], recv_sem.at[0])
    nodes01 = Exchange(me, part01, got01, 8, send_sem.at[1], recv_sem.at[1])
    nodes2 = Exchange(me, part2, got2, 4, send_sem.at[2], recv_sem.at[2])
    fringes.keep()
    halos = []
    for side, to in ((0, lax.rem(dom + DOMS - 1, DOMS)), (1, lax.rem(dom + 1, DOMS))):
        copy = pltpu.make_async_remote_copy(
            src_ref=halo_out.at[side],
            dst_ref=halo_in.at[side],
            send_sem=halo_send.at[side],
            recv_sem=halo_recv.at[side],
            device_id=(to, grid),
            device_id_type=MESH,
        )
        copy.start()
        halos.append(copy)

    load_met.wait()

    def corners(block, peaks):
        rows8 = pl.ds(block * 8, 8)
        values = [adj[i, rows8, :] for i in range(6)]
        found = []
        for x in range(3):
            peak = peaks[x]
            for k in range(4):
                term = met[0, x, k, rows8, :] * values[0]
                for i in range(1, 6):
                    term = term + met[i, x, k, rows8, :] * values[i]
                met[0, x, k, rows8, :] = term
                peak = jnp.maximum(peak, jnp.abs(term))
            found.append(peak)
        return tuple(found)

    peaks = lax.fori_loop(0, 16, corners, (jnp.zeros((8, 128), F32),) * 3)
    peaks = [jnp.maximum(jnp.max(peak, keepdims=True), 1e-30) for peak in peaks]

    depth = 4
    zero64 = jnp.zeros((64, 128), BF)
    ids8 = (lax.broadcasted_iota(jnp.int32, (256, 128), 0) - 128).astype(jnp.int8)
    one8, zero8 = jnp.ones((), F8), jnp.zeros((), F8)

    def node_pass(xs, exchange):
        for t in range(3 * len(xs)):
            acc[t] = jnp.zeros((256, 256), F32)
        scales = [jnp.broadcast_to(440.0 / peaks[x], (8, 128)) for x in xs]

        def tile(step, carry):
            exchange.send(2 * step + 1)
            exchange.send(2 * step + 2)
            k, rows8 = lax.div(step, 16), pl.ds(lax.rem(step, 16) * 8, 8)
            n = nid[k, rows8, :]
            high = ((n >> 8) & 1) * 128 + (n >> 9) - 128
            low = (n & 255) - 128
            terms = []
            for x, scale in zip(xs, scales):
                terms += digits(met[0, x, k, rows8, :] * scale)
            for group in range(8 // depth):
                js = range(group * depth, (group + 1) * depth)
                lows = jnp.concatenate(
                    [jnp.where(ids8 == spread8(low[j:j + 1], jnp.int8), one8, zero8) for j in js], 1
                )
                masks = [ids8 == spread8(high[j:j + 1], jnp.int8) for j in js]
                for t in range(3 * len(xs)):
                    highs = jnp.concatenate(
                        [jnp.where(m, spread8(terms[t][j:j + 1], F8), zero8) for m, j in zip(masks, js)], 1
                    )
                    acc[t] += lax.dot_general(
                        highs, lows, (((1,), (1,)), ((), ())), preferred_element_type=F32
                    )
            return carry

        lax.fori_loop(0, 64, tile, 0)

    def node_store(where, xs):
        for slot, x in enumerate(xs):
            unit = peaks[x] * (1.0 / 440.0)
            for e in range(2):
                rows = slice(e * 128, (e + 1) * 128)
                total = acc[3 * slot + 1, rows, :] + acc[3 * slot + 2, rows, :] * (1.0 / 16.0)
                total = (acc[3 * slot, rows, :] + total * (1.0 / 16.0)) * unit
                for b in range(2):
                    where[0:128, slot * 4 + e * 2 + b, :] = total[:, b * 128:(b + 1) * 128]

    node_pass((0, 1), fringes)
    node_store(part01, (0, 1))
    nodes01.keep()
    node_pass((2,), nodes01)
    node_store(part2, (2,))
    nodes2.keep()

    fringes.wait_recv()
    for t in range(3):
        acc[t] = jnp.zeros((256, 256), F32)

    def senders(block, carry):
        for k in range(8):
            nodes2.send(block * 8 + k + 1)
        rows8 = pl.ds(block * 8, 8)
        cells = donor[rows8, :]
        rows, cols = cells >> 7, cells & 127
        high = (rows & 63).astype(F32)
        low = ((rows >> 6) * 128 + cols).astype(F32)
        live = lane_ids[0:8].astype(F32) < counts[rows8, :]
        weights = jnp.where(live, weight[rows8, :], 0.0)
        values = [halves(-(recv[rows8, i, :] * weights)) for i in range(6)]
        for group in range(8 // depth):
            js = range(group * depth, (group + 1) * depth)
            lows = jnp.concatenate([onehot(ids256 == spread(low[j:j + 1], 256)) for j in js], 1)
            masks = [ids64 == spread(high[j:j + 1], 64) for j in js]
            for third in range(3):
                highs = jnp.concatenate(
                    [
                        jnp.concatenate(
                            [jnp.where(m, spread(values[i][half][j:j + 1], 64), zero64) for m, j in zip(masks, js)],
                            1,
                        )
                        for i in (2 * third, 2 * third + 1)
                        for half in range(2)
                    ],
                    0,
                )
                acc[third] += lax.dot_general(
                    highs, lows, (((1,), (1,)), ((), ())), preferred_element_type=F32
                )
        return carry

    lax.fori_loop(0, 16, senders, 0)
    for i in range(6):
        start = (i % 2) * 128
        both = acc[i // 2, start:start + 64, :] + acc[i // 2, start + 64:start + 128, :]
        product[i, :64, :] = both[:, :128]
        product[i, 64:, :] = both[:, 128:]

    load_diag.wait()
    for copy in halos:
        copy.wait()
    first, last = row_ids == 0, row_ids == 127
    left, right = lane_ids == 0, lane_ids == 127

    def variable(j, carry):
        def against(block):
            total = block(0) * adj[0]
            for i in range(1, 6):
                total = total + block(i) * adj[i]
            return total

        below = jnp.where(dom == DOMS - 1, 0.0, halo_in[0, pl.ds(j, 1), :])
        above = jnp.where(dom == 0, 0.0, halo_in[1, pl.ds(j, 1), :])
        total = product[j] + against(lambda i: diag[i, j])
        up = pltpu.roll(against(lambda i: face[i, 0, j]), 127, 0)
        total = total + jnp.where(last, jnp.broadcast_to(below, (128, 128)), up)
        down = pltpu.roll(against(lambda i: face[i, 1, j]), 1, 0)
        total = total + jnp.where(first, jnp.broadcast_to(above, (128, 128)), down)
        total = total + jnp.where(right, 0.0, pltpu.roll(against(lambda i: face[i, 2, j]), 127, 1))
        total = total + jnp.where(left, 0.0, pltpu.roll(against(lambda i: face[i, 3, j]), 1, 1))
        product[j] = total
        return carry

    lax.fori_loop(0, 6, variable, 0)

    nodes01.wait_recv()
    owned = jnp.sum(got01[0:128], axis=0)
    for x in range(2):
        for b in range(4):
            sens[x:x + 1, b * 128:(b + 1) * 128] = owned[x * 4 + b:x * 4 + b + 1, :]
    nodes2.wait_recv()
    owned = jnp.sum(got2[0:128, 0:4, :], axis=0)
    for b in range(4):
        sens[2:3, b * 128:(b + 1) * 128] = owned[b:b + 1, :]

    for exchange in (fringes, nodes01, nodes2):
        exchange.wait_send()


def local(
    adjoint, jac_diag, jac_face, metric, node_id, fringe_cell, donor_cell, fringe_weight, donor_count
):
    vmem = pl.BlockSpec(memory_space=pltpu.VMEM)
    hbm = pl.BlockSpec(memory_space=pl.ANY)
    source = pltpu.VMEM((DEVICES, 8, 128), F32)
    target = pltpu.VMEM((DEVICES + 1, 8, 128), F32)
    product, sens = pl.pallas_call(
        kernel,
        in_specs=[vmem] * 6 + [hbm] * 3,
        out_specs=[vmem, vmem],
        out_shape=[
            jax.ShapeDtypeStruct((6, 128, 128), F32),
            jax.ShapeDtypeStruct((3, 512), F32),
        ],
        scratch_shapes=[
            pltpu.VMEM((6, 6, 128, 128), F32),
            pltpu.VMEM((6, 4, 6, 128, 128), F32),
            pltpu.VMEM((6, 3, 4, 128, 128), F32),
            pltpu.VMEM((768, 256), BF),
            pltpu.VMEM((128, 128), F32),
            pltpu.VMEM((6, 256, 256), F32),
            source, target, source, target, source, target,
            pltpu.VMEM((2, 8, 128), F32),
            pltpu.VMEM((2, 8, 128), F32),
            pltpu.SemaphoreType.DMA((3,)),
            pltpu.SemaphoreType.DMA((3,)),
            pltpu.SemaphoreType.DMA((3,)),
            pltpu.SemaphoreType.DMA((2,)),
            pltpu.SemaphoreType.DMA((2,)),
        ],
        compiler_params=pltpu.CompilerParams(
            collective_id=0, has_side_effects=True, vmem_limit_bytes=58 * 2**20
        ),
        name="adjoint_step",
    )(
        adjoint[0], fringe_cell[0], node_id[0], donor_cell[0], fringe_weight[0], donor_count,
        jac_diag[0], jac_face[0], metric[0],
    )
    return (product[None], sens)


def solution(mesh):
    in_specs = (
        P("grid", None, "dom", None),
        P("grid", None, None, "dom", None),
        P("grid", None, None, None, "dom", None),
        P("grid", None, None, None, "dom", None),
        P("grid", None, "dom", None),
        P(("dom", "grid"), None, None),
        P(("dom", "grid"), None, None),
        P(("dom", "grid"), None, None),
        P(("dom", "grid"), None),
    )
    out_specs = (P("grid", None, "dom", None), P(None, ("dom", "grid")))
    return jax.shard_map(local, mesh=mesh, in_specs=in_specs, out_specs=out_specs, check_vma=False)
```

```python
import jax
import jax.numpy as jnp
from jax import lax
from jax.experimental import pallas as pl
from jax.experimental.pallas import tpu as pltpu
from jax.sharding import PartitionSpec as P

BF = jnp.bfloat16
F8 = jnp.float8_e4m3fn
F32 = jnp.float32
NODE_DEPTH = 8
DONOR_DEPTH = 8
FRINGE_STEP = 2
DONOR_STEP = 4
NODE_STEP = 2
DEVICES = 128
GRIDS = 8
DOMS = 16
MESH = pl.DeviceIdType.MESH


def spread(row, rows):
    tile = jnp.broadcast_to(row, (16, row.shape[1])).astype(BF)
    return jnp.concatenate([tile] * (rows // 16), axis=0)


def spread8(row, kind):
    tile = jnp.broadcast_to(row, (32, row.shape[1])).astype(kind)
    return jnp.concatenate([tile] * 8, axis=0)


def digits(value):
    first = value.astype(F8).astype(F32)
    rest = (value - first) * 16.0
    second = rest.astype(F8).astype(F32)
    return first, second, (rest - second) * 16.0


def ids(rows):
    return lax.broadcasted_iota(jnp.int32, (rows, 128), 0).astype(F32).astype(BF)


def halves(value):
    high = value.astype(BF).astype(F32)
    return high, value - high


def onehot(mask):
    return jnp.where(mask, jnp.ones((), BF), jnp.zeros((), BF))


def partner(me, step):
    device = me + jnp.where(step == DEVICES, DEVICES // 2, step)
    device = jnp.where(device >= DEVICES, device - DEVICES, device)
    return device, (lax.div(device, GRIDS), lax.rem(device, GRIDS))


def wait_for(view, semaphore):
    pltpu.make_async_copy(view, view, semaphore).wait()


class Exchange:
    def __init__(self, me, source, target, rows, send_sem, recv_sem):
        self.me, self.source, self.target, self.rows = me, source, target, rows
        self.send_sem, self.recv_sem = send_sem, recv_sem

    def block(self, ref, index):
        return ref.at[index] if self.rows == 8 else ref.at[index, pl.ds(0, self.rows)]

    def keep(self):
        pltpu.make_async_copy(
            self.block(self.source, self.me), self.block(self.target, self.me), self.recv_sem
        ).start()

    def send(self, step):
        device, coordinates = partner(self.me, step)
        pltpu.make_async_remote_copy(
            src_ref=self.block(self.source, device),
            dst_ref=self.block(self.target, jnp.where(step == DEVICES, DEVICES, self.me)),
            send_sem=self.send_sem,
            recv_sem=self.recv_sem,
            device_id=coordinates,
            device_id_type=MESH,
        ).start()

    def wait_recv(self):
        wait_for(self.block(self.target, pl.ds(0, DEVICES + 1)), self.recv_sem)

    def wait_send(self):
        wait_for(self.block(self.source, pl.ds(0, DEVICES)), self.send_sem)


def kernel(
    adj, cell, nid, donor, weight, count, diag_hbm, face_hbm, met_hbm,
    product, sens,
    diag, face, met, table, counts, acc,
    pay, recv, part01, got01, part2, got2, halo_out, halo_in,
    local_sem, send_sem, recv_sem, halo_send, halo_recv,
):
    dom, grid = lax.axis_index("dom"), lax.axis_index("grid")
    me = dom * GRIDS + grid
    load_face = pltpu.make_async_copy(face_hbm, face, local_sem.at[0])
    load_met = pltpu.make_async_copy(met_hbm, met, local_sem.at[1])
    load_diag = pltpu.make_async_copy(diag_hbm, diag, local_sem.at[2])
    load_face.start()
    load_met.start()
    load_diag.start()
    barrier = pltpu.get_barrier_semaphore()

    for v in range(6):
        high, low = halves(adj[v])
        table[v * 128:(v + 1) * 128, :128] = high.astype(BF)
        table[v * 128:(v + 1) * 128, 128:] = low.astype(BF)
    counts[...] = jnp.broadcast_to(count[...].astype(F32), (128, 128)).T
    ids64, ids128, ids256 = ids(64), ids(128), ids(256)
    row_ids = lax.broadcasted_iota(jnp.int32, (128, 128), 0)
    lane_ids = lax.broadcasted_iota(jnp.int32, (128, 128), 1)
    sublanes = lax.broadcasted_iota(jnp.int32, (8, 128), 0)

    def fringe(step, carry):
        for k in range(8 * FRINGE_STEP):
            pl.semaphore_signal(
                barrier, inc=1, device_id=partner(me, step * 8 * FRINGE_STEP + k + 1)[1], device_id_type=MESH
            )
        for u in range(FRINGE_STEP):
            fringe_rows(step * FRINGE_STEP + u)
        return carry

    def fringe_rows(block):
        cells = cell[pl.ds(block * 8, 8), :]
        rows, lanes = cells >> 7, (cells & 127).astype(F32)
        for pair in range(4):
            js = (2 * pair, 2 * pair + 1)
            pick = jnp.concatenate([onehot(ids128 == spread(lanes[j:j + 1], 128)) for j in js], 1)
            pick = jnp.concatenate([pick, pick], 0)
            wide = [jnp.broadcast_to(rows[j:j + 1], (8, 128)) for j in js]
            bands = [[(w >> 3) == band for band in range(16)] for w in wide]
            hits = [sublanes == (w & 7) for w in wide]
            found = jnp.dot(table[...], pick, preferred_element_type=F32)
            for v in range(6):
                for side, j in enumerate(js):
                    columns = slice(side * 128, (side + 1) * 128)
                    mine = found[v * 128:v * 128 + 8, columns]
                    for band in range(1, 16):
                        start = v * 128 + band * 8
                        mine = jnp.where(bands[side][band], found[start:start + 8, columns], mine)
                    mine = jnp.where(hits[side], mine, 0.0)
                    pay[block * 8 + j, v:v + 1, :] = jnp.sum(mine, axis=0, keepdims=True)

    lax.fori_loop(0, 16 // FRINGE_STEP, fringe, 0)

    load_face.wait()
    for side, row in ((0, 0), (1, 127)):
        edge = face[0, side, :, row, :] * adj[0, row:row + 1, :]
        for i in range(1, 6):
            edge = edge + face[i, side, :, row, :] * adj[i, row:row + 1, :]
        halo_out[side, 0:6, :] = edge

    pl.semaphore_wait(barrier, DEVICES)
    fringes = Exchange(me, pay, recv, 8, send_sem.at[0], recv_sem.at[0])
    nodes01 = Exchange(me, part01, got01, 8, send_sem.at[1], recv_sem.at[1])
    nodes2 = Exchange(me, part2, got2, 4, send_sem.at[2], recv_sem.at[2])
    fringes.keep()
    halos = []
    for side, to in ((0, lax.rem(dom + DOMS - 1, DOMS)), (1, lax.rem(dom + 1, DOMS))):
        copy = pltpu.make_async_remote_copy(
            src_ref=halo_out.at[side],
            dst_ref=halo_in.at[side],
            send_sem=halo_send.at[side],
            recv_sem=halo_recv.at[side],
            device_id=(to, grid),
            device_id_type=MESH,
        )
        copy.start()
        halos.append(copy)

    load_met.wait()

    def corners(block, peaks):
        rows8 = pl.ds(block * 8, 8)
        values = [adj[i, rows8, :] for i in range(6)]
        found = []
        for x in range(3):
            peak = peaks[x]
            for k in range(4):
                term = met[0, x, k, rows8, :] * values[0]
                for i in range(1, 6):
                    term = term + met[i, x, k, rows8, :] * values[i]
                met[0, x, k, rows8, :] = term
                peak = jnp.maximum(peak, jnp.abs(term))
            found.append(peak)
        return tuple(found)

    peaks = lax.fori_loop(0, 16, corners, (jnp.zeros((8, 128), F32),) * 3)
    peaks = [jnp.maximum(jnp.max(peak, keepdims=True), 1e-30) for peak in peaks]

    zero64 = jnp.zeros((64, 128), BF)
    ids8 = (lax.broadcasted_iota(jnp.int32, (256, 128), 0) - 128).astype(jnp.int8)
    one8, zero8 = jnp.ones((), F8), jnp.zeros((), F8)

    def node_pass(xs, exchange):
        for t in range(3 * len(xs)):
            acc[t] = jnp.zeros((256, 256), F32)
        scales = [jnp.broadcast_to(440.0 / peaks[x], (8, 128)) for x in xs]

        def tile(step, carry):
            for k in range(8 * NODE_STEP):
                exchange.send(8 * NODE_STEP * step + k + 1)
            for u in range(NODE_STEP):
                for k in range(4):
                    corner(k, pl.ds((step * NODE_STEP + u) * 8, 8))
            return carry

        def corner(k, rows8):
            n = nid[k, rows8, :]
            high = ((n >> 8) & 1) * 128 + (n >> 9) - 128
            low = (n & 255) - 128
            terms = []
            for x, scale in zip(xs, scales):
                terms += digits(met[0, x, k, rows8, :] * scale)
            for group in range(8 // NODE_DEPTH):
                js = range(group * NODE_DEPTH, (group + 1) * NODE_DEPTH)
                lows = jnp.concatenate(
                    [jnp.where(ids8 == spread8(low[j:j + 1], jnp.int8), one8, zero8) for j in js], 1
                )
                masks = [ids8 == spread8(high[j:j + 1], jnp.int8) for j in js]
                for t in range(3 * len(xs)):
                    highs = jnp.concatenate(
                        [jnp.where(m, spread8(terms[t][j:j + 1], F8), zero8) for m, j in zip(masks, js)], 1
                    )
                    acc[t] += lax.dot_general(
                        highs, lows, (((1,), (1,)), ((), ())), preferred_element_type=F32
                    )

        lax.fori_loop(0, 16 // NODE_STEP, tile, 0)

    def node_store(where, xs):
        for slot, x in enumerate(xs):
            unit = peaks[x] * (1.0 / 440.0)
            for e in range(2):
                rows = slice(e * 128, (e + 1) * 128)
                total = acc[3 * slot + 1, rows, :] + acc[3 * slot + 2, rows, :] * (1.0 / 16.0)
                total = (acc[3 * slot, rows, :] + total * (1.0 / 16.0)) * unit
                for b in range(2):
                    where[0:128, slot * 4 + e * 2 + b, :] = total[:, b * 128:(b + 1) * 128]

    node_pass((0, 1), fringes)
    node_store(part01, (0, 1))
    nodes01.keep()
    node_pass((2,), nodes01)
    node_store(part2, (2,))
    nodes2.keep()

    fringes.wait_recv()
    for t in range(3):
        acc[t] = jnp.zeros((256, 256), F32)

    def senders(step, carry):
        for k in range(8 * DONOR_STEP):
            nodes2.send(step * 8 * DONOR_STEP + k + 1)
        for u in range(DONOR_STEP):
            donors(step * DONOR_STEP + u)
        return carry

    def donors(block):
        rows8 = pl.ds(block * 8, 8)
        cells = donor[rows8, :]
        rows, cols = cells >> 7, cells & 127
        high = (rows & 63).astype(F32)
        low = ((rows >> 6) * 128 + cols).astype(F32)
        live = lane_ids[0:8].astype(F32) < counts[rows8, :]
        weights = jnp.where(live, weight[rows8, :], 0.0)
        values = [halves(-(recv[rows8, i, :] * weights)) for i in range(6)]
        for group in range(8 // DONOR_DEPTH):
            js = range(group * DONOR_DEPTH, (group + 1) * DONOR_DEPTH)
            lows = jnp.concatenate([onehot(ids256 == spread(low[j:j + 1], 256)) for j in js], 1)
            masks = [ids64 == spread(high[j:j + 1], 64) for j in js]
            for third in range(3):
                highs = jnp.concatenate(
                    [
                        jnp.concatenate(
                            [jnp.where(m, spread(values[i][half][j:j + 1], 64), zero64) for m, j in zip(masks, js)],
                            1,
                        )
                        for i in (2 * third, 2 * third + 1)
                        for half in range(2)
                    ],
                    0,
                )
                acc[third] += lax.dot_general(
                    highs, lows, (((1,), (1,)), ((), ())), preferred_element_type=F32
                )

    lax.fori_loop(0, 16 // DONOR_STEP, senders, 0)
    for i in range(6):
        start = (i % 2) * 128
        both = acc[i // 2, start:start + 64, :] + acc[i // 2, start + 64:start + 128, :]
        product[i, :64, :] = both[:, :128]
        product[i, 64:, :] = both[:, 128:]

    load_diag.wait()
    for copy in halos:
        copy.wait()
    first, last = row_ids == 0, row_ids == 127
    left, right = lane_ids == 0, lane_ids == 127

    def variable(j, carry):
        def against(block):
            total = block(0) * adj[0]
            for i in range(1, 6):
                total = total + block(i) * adj[i]
            return total

        below = jnp.where(dom == DOMS - 1, 0.0, halo_in[0, pl.ds(j, 1), :])
        above = jnp.where(dom == 0, 0.0, halo_in[1, pl.ds(j, 1), :])
        total = product[j] + against(lambda i: diag[i, j])
        up = pltpu.roll(against(lambda i: face[i, 0, j]), 127, 0)
        total = total + jnp.where(last, jnp.broadcast_to(below, (128, 128)), up)
        down = pltpu.roll(against(lambda i: face[i, 1, j]), 1, 0)
        total = total + jnp.where(first, jnp.broadcast_to(above, (128, 128)), down)
        total = total + jnp.where(right, 0.0, pltpu.roll(against(lambda i: face[i, 2, j]), 127, 1))
        total = total + jnp.where(left, 0.0, pltpu.roll(against(lambda i: face[i, 3, j]), 1, 1))
        product[j] = total
        return carry

    lax.fori_loop(0, 6, variable, 0)

    nodes01.wait_recv()
    owned = jnp.sum(got01[0:128], axis=0)
    for x in range(2):
        for b in range(4):
            sens[x:x + 1, b * 128:(b + 1) * 128] = owned[x * 4 + b:x * 4 + b + 1, :]
    nodes2.wait_recv()
    owned = jnp.sum(got2[0:128, 0:4, :], axis=0)
    for b in range(4):
        sens[2:3, b * 128:(b + 1) * 128] = owned[b:b + 1, :]

    for exchange in (fringes, nodes01, nodes2):
        exchange.wait_send()


def local(
    adjoint, jac_diag, jac_face, metric, node_id, fringe_cell, donor_cell, fringe_weight, donor_count
):
    vmem = pl.BlockSpec(memory_space=pltpu.VMEM)
    hbm = pl.BlockSpec(memory_space=pl.ANY)
    source = pltpu.VMEM((DEVICES, 8, 128), F32)
    target = pltpu.VMEM((DEVICES + 1, 8, 128), F32)
    product, sens = pl.pallas_call(
        kernel,
        in_specs=[vmem] * 6 + [hbm] * 3,
        out_specs=[vmem, vmem],
        out_shape=[
            jax.ShapeDtypeStruct((6, 128, 128), F32),
            jax.ShapeDtypeStruct((3, 512), F32),
        ],
        scratch_shapes=[
            pltpu.VMEM((6, 6, 128, 128), F32),
            pltpu.VMEM((6, 4, 6, 128, 128), F32),
            pltpu.VMEM((6, 3, 4, 128, 128), F32),
            pltpu.VMEM((768, 256), BF),
            pltpu.VMEM((128, 128), F32),
            pltpu.VMEM((6, 256, 256), F32),
            source, target, source, target, source, target,
            pltpu.VMEM((2, 8, 128), F32),
            pltpu.VMEM((2, 8, 128), F32),
            pltpu.SemaphoreType.DMA((3,)),
            pltpu.SemaphoreType.DMA((3,)),
            pltpu.SemaphoreType.DMA((3,)),
            pltpu.SemaphoreType.DMA((2,)),
            pltpu.SemaphoreType.DMA((2,)),
        ],
        compiler_params=pltpu.CompilerParams(
            collective_id=0, has_side_effects=True, vmem_limit_bytes=58 * 2**20
        ),
        name="adjoint_step",
    )(
        adjoint[0], fringe_cell[0], node_id[0], donor_cell[0], fringe_weight[0], donor_count,
        jac_diag[0], jac_face[0], metric[0],
    )
    return (product[None], sens)


def solution(mesh):
    in_specs = (
        P("grid", None, "dom", None),
        P("grid", None, None, "dom", None),
        P("grid", None, None, None, "dom", None),
        P("grid", None, None, None, "dom", None),
        P("grid", None, "dom", None),
        P(("dom", "grid"), None, None),
        P(("dom", "grid"), None, None),
        P(("dom", "grid"), None, None),
        P(("dom", "grid"), None),
    )
    out_specs = (P("grid", None, "dom", None), P(None, ("dom", "grid")))
    return jax.shard_map(local, mesh=mesh, in_specs=in_specs, out_specs=out_specs, check_vma=False)
```

```python
import jax
import jax.numpy as jnp
from jax import lax
from jax.experimental import pallas as pl
from jax.experimental.pallas import tpu as pltpu
from jax.sharding import PartitionSpec as P

BF = jnp.bfloat16
F8 = jnp.float8_e4m3fn
F32 = jnp.float32
NODE_DEPTH = 8
DONOR_DEPTH = 8
FRINGE_STEP = 4
DONOR_STEP = 8
NODE_STEP = 4
DEVICES = 128
GRIDS = 8
DOMS = 16
MESH = pl.DeviceIdType.MESH


def spread(row, rows):
    tile = jnp.broadcast_to(row, (16, row.shape[1])).astype(BF)
    return jnp.concatenate([tile] * (rows // 16), axis=0)


def spread8(row, kind):
    tile = jnp.broadcast_to(row, (32, row.shape[1])).astype(kind)
    return jnp.concatenate([tile] * 8, axis=0)


def digits(value):
    first = value.astype(F8).astype(F32)
    rest = (value - first) * 16.0
    second = rest.astype(F8).astype(F32)
    return first, second, (rest - second) * 16.0


def ids(rows):
    return lax.broadcasted_iota(jnp.int32, (rows, 128), 0).astype(F32).astype(BF)


def halves(value):
    high = value.astype(BF).astype(F32)
    return high, value - high


def onehot(mask):
    return jnp.where(mask, jnp.ones((), BF), jnp.zeros((), BF))


def partner(me, step):
    device = me + jnp.where(step == DEVICES, DEVICES // 2, step)
    device = jnp.where(device >= DEVICES, device - DEVICES, device)
    return device, (lax.div(device, GRIDS), lax.rem(device, GRIDS))


def wait_for(view, semaphore):
    pltpu.make_async_copy(view, view, semaphore).wait()


class Exchange:
    def __init__(self, me, source, target, rows, send_sem, recv_sem):
        self.me, self.source, self.target, self.rows = me, source, target, rows
        self.send_sem, self.recv_sem = send_sem, recv_sem

    def block(self, ref, index):
        return ref.at[index] if self.rows == 8 else ref.at[index, pl.ds(0, self.rows)]

    def keep(self):
        pltpu.make_async_copy(
            self.block(self.source, self.me), self.block(self.target, self.me), self.recv_sem
        ).start()

    def send(self, step):
        device, coordinates = partner(self.me, step)
        pltpu.make_async_remote_copy(
            src_ref=self.block(self.source, device),
            dst_ref=self.block(self.target, jnp.where(step == DEVICES, DEVICES, self.me)),
            send_sem=self.send_sem,
            recv_sem=self.recv_sem,
            device_id=coordinates,
            device_id_type=MESH,
        ).start()

    def wait_recv(self):
        wait_for(self.block(self.target, pl.ds(0, DEVICES + 1)), self.recv_sem)

    def wait_send(self):
        wait_for(self.block(self.source, pl.ds(0, DEVICES)), self.send_sem)


def kernel(
    adj, cell, nid, donor, weight, count, diag_hbm, face_hbm, met_hbm,
    product, sens,
    diag, face, met, table, counts, acc,
    pay, recv, part01, got01, part2, got2, halo_out, halo_in,
    local_sem, send_sem, recv_sem, halo_send, halo_recv,
):
    dom, grid = lax.axis_index("dom"), lax.axis_index("grid")
    me = dom * GRIDS + grid
    load_face = pltpu.make_async_copy(face_hbm, face, local_sem.at[0])
    load_met = pltpu.make_async_copy(met_hbm, met, local_sem.at[1])
    load_diag = pltpu.make_async_copy(diag_hbm, diag, local_sem.at[2])
    load_face.start()
    load_met.start()
    load_diag.start()
    barrier = pltpu.get_barrier_semaphore()

    def greet(step, carry):
        for k in range(16):
            pl.semaphore_signal(
                barrier, inc=1, device_id=partner(me, step * 16 + k + 1)[1], device_id_type=MESH
            )
        return carry

    lax.fori_loop(0, 8, greet, 0)

    for v in range(6):
        high, low = halves(adj[v])
        table[v * 128:(v + 1) * 128, :128] = high.astype(BF)
        table[v * 128:(v + 1) * 128, 128:] = low.astype(BF)
    counts[...] = jnp.broadcast_to(count[...].astype(F32), (128, 128)).T
    ids64, ids128, ids256 = ids(64), ids(128), ids(256)
    row_ids = lax.broadcasted_iota(jnp.int32, (128, 128), 0)
    lane_ids = lax.broadcasted_iota(jnp.int32, (128, 128), 1)
    sublanes = lax.broadcasted_iota(jnp.int32, (8, 128), 0)

    def fringe(step, carry):
        for u in range(FRINGE_STEP):
            fringe_rows(step * FRINGE_STEP + u)
        return carry

    def fringe_rows(block):
        cells = cell[pl.ds(block * 8, 8), :]
        rows, lanes = cells >> 7, (cells & 127).astype(F32)
        for pair in range(4):
            js = (2 * pair, 2 * pair + 1)
            pick = jnp.concatenate([onehot(ids128 == spread(lanes[j:j + 1], 128)) for j in js], 1)
            pick = jnp.concatenate([pick, pick], 0)
            wide = [jnp.broadcast_to(rows[j:j + 1], (8, 128)) for j in js]
            bands = [[(w >> 3) == band for band in range(16)] for w in wide]
            hits = [sublanes == (w & 7) for w in wide]
            found = jnp.dot(table[...], pick, preferred_element_type=F32)
            for v in range(6):
                for side, j in enumerate(js):
                    columns = slice(side * 128, (side + 1) * 128)
                    mine = found[v * 128:v * 128 + 8, columns]
                    for band in range(1, 16):
                        start = v * 128 + band * 8
                        mine = jnp.where(bands[side][band], found[start:start + 8, columns], mine)
                    mine = jnp.where(hits[side], mine, 0.0)
                    pay[block * 8 + j, v:v + 1, :] = jnp.sum(mine, axis=0, keepdims=True)

    lax.fori_loop(0, 16 // FRINGE_STEP, fringe, 0)

    load_face.wait()
    for side, row in ((0, 0), (1, 127)):
        edge = face[0, side, :, row, :] * adj[0, row:row + 1, :]
        for i in range(1, 6):
            edge = edge + face[i, side, :, row, :] * adj[i, row:row + 1, :]
        halo_out[side, 0:6, :] = edge

    load_met.wait()

    def corners(block, peaks):
        rows8 = pl.ds(block * 8, 8)
        values = [adj[i, rows8, :] for i in range(6)]
        found = []
        for x in range(3):
            peak = peaks[x]
            for k in range(4):
                term = met[0, x, k, rows8, :] * values[0]
                for i in range(1, 6):
                    term = term + met[i, x, k, rows8, :] * values[i]
                met[0, x, k, rows8, :] = term
                peak = jnp.maximum(peak, jnp.abs(term))
            found.append(peak)
        return tuple(found)

    peaks = lax.fori_loop(0, 16, corners, (jnp.zeros((8, 128), F32),) * 3)
    peaks = [jnp.maximum(jnp.max(peak, keepdims=True), 1e-30) for peak in peaks]

    pl.semaphore_wait(barrier, DEVICES)
    fringes = Exchange(me, pay, recv, 8, send_sem.at[0], recv_sem.at[0])
    nodes01 = Exchange(me, part01, got01, 8, send_sem.at[1], recv_sem.at[1])
    nodes2 = Exchange(me, part2, got2, 4, send_sem.at[2], recv_sem.at[2])
    fringes.keep()
    halos = []
    for side, to in ((0, lax.rem(dom + DOMS - 1, DOMS)), (1, lax.rem(dom + 1, DOMS))):
        copy = pltpu.make_async_remote_copy(
            src_ref=halo_out.at[side],
            dst_ref=halo_in.at[side],
            send_sem=halo_send.at[side],
            recv_sem=halo_recv.at[side],
            device_id=(to, grid),
            device_id_type=MESH,
        )
        copy.start()
        halos.append(copy)

    zero64 = jnp.zeros((64, 128), BF)
    ids8 = (lax.broadcasted_iota(jnp.int32, (256, 128), 0) - 128).astype(jnp.int8)
    one8, zero8 = jnp.ones((), F8), jnp.zeros((), F8)

    def node_pass(xs, exchange):
        for t in range(3 * len(xs)):
            acc[t] = jnp.zeros((256, 256), F32)
        scales = [jnp.broadcast_to(440.0 / peaks[x], (8, 128)) for x in xs]

        def tile(step, carry):
            for k in range(8 * NODE_STEP):
                exchange.send(8 * NODE_STEP * step + k + 1)
            for u in range(NODE_STEP):
                for k in range(4):
                    corner(k, pl.ds((step * NODE_STEP + u) * 8, 8))
            return carry

        def corner(k, rows8):
            n = nid[k, rows8, :]
            high = ((n >> 8) & 1) * 128 + (n >> 9) - 128
            low = (n & 255) - 128
            terms = []
            for x, scale in zip(xs, scales):
                terms += digits(met[0, x, k, rows8, :] * scale)
            for group in range(8 // NODE_DEPTH):
                js = range(group * NODE_DEPTH, (group + 1) * NODE_DEPTH)
                lows = jnp.concatenate(
                    [jnp.where(ids8 == spread8(low[j:j + 1], jnp.int8), one8, zero8) for j in js], 1
                )
                masks = [ids8 == spread8(high[j:j + 1], jnp.int8) for j in js]
                for t in range(3 * len(xs)):
                    highs = jnp.concatenate(
                        [jnp.where(m, spread8(terms[t][j:j + 1], F8), zero8) for m, j in zip(masks, js)], 1
                    )
                    acc[t] += lax.dot_general(
                        highs, lows, (((1,), (1,)), ((), ())), preferred_element_type=F32
                    )

        lax.fori_loop(0, 16 // NODE_STEP, tile, 0)

    def node_store(where, xs):
        for slot, x in enumerate(xs):
            unit = peaks[x] * (1.0 / 440.0)
            for e in range(2):
                rows = slice(e * 128, (e + 1) * 128)
                total = acc[3 * slot + 1, rows, :] + acc[3 * slot + 2, rows, :] * (1.0 / 16.0)
                total = (acc[3 * slot, rows, :] + total * (1.0 / 16.0)) * unit
                for b in range(2):
                    where[0:128, slot * 4 + e * 2 + b, :] = total[:, b * 128:(b + 1) * 128]

    node_pass((0, 1), fringes)
    node_store(part01, (0, 1))
    nodes01.keep()
    node_pass((2,), nodes01)
    node_store(part2, (2,))
    nodes2.keep()

    fringes.wait_recv()
    for t in range(3):
        acc[t] = jnp.zeros((256, 256), F32)

    def senders(step, carry):
        for k in range(8 * DONOR_STEP):
            nodes2.send(step * 8 * DONOR_STEP + k + 1)
        for u in range(DONOR_STEP):
            donors(step * DONOR_STEP + u)
        return carry

    def donors(block):
        rows8 = pl.ds(block * 8, 8)
        cells = donor[rows8, :]
        rows, cols = cells >> 7, cells & 127
        high = (rows & 63).astype(F32)
        low = ((rows >> 6) * 128 + cols).astype(F32)
        live = lane_ids[0:8].astype(F32) < counts[rows8, :]
        weights = jnp.where(live, weight[rows8, :], 0.0)
        values = [halves(-(recv[rows8, i, :] * weights)) for i in range(6)]
        for group in range(8 // DONOR_DEPTH):
            js = range(group * DONOR_DEPTH, (group + 1) * DONOR_DEPTH)
            lows = jnp.concatenate([onehot(ids256 == spread(low[j:j + 1], 256)) for j in js], 1)
            masks = [ids64 == spread(high[j:j + 1], 64) for j in js]
            for third in range(3):
                highs = jnp.concatenate(
                    [
                        jnp.concatenate(
                            [jnp.where(m, spread(values[i][half][j:j + 1], 64), zero64) for m, j in zip(masks, js)],
                            1,
                        )
                        for i in (2 * third, 2 * third + 1)
                        for half in range(2)
                    ],
                    0,
                )
                acc[third] += lax.dot_general(
                    highs, lows, (((1,), (1,)), ((), ())), preferred_element_type=F32
                )

    lax.fori_loop(0, 16 // DONOR_STEP, senders, 0)
    for i in range(6):
        start = (i % 2) * 128
        both = acc[i // 2, start:start + 64, :] + acc[i // 2, start + 64:start + 128, :]
        product[i, :64, :] = both[:, :128]
        product[i, 64:, :] = both[:, 128:]

    load_diag.wait()
    for copy in halos:
        copy.wait()
    first, last = row_ids == 0, row_ids == 127
    left, right = lane_ids == 0, lane_ids == 127

    def variable(j, carry):
        def against(block):
            total = block(0) * adj[0]
            for i in range(1, 6):
                total = total + block(i) * adj[i]
            return total

        below = jnp.where(dom == DOMS - 1, 0.0, halo_in[0, pl.ds(j, 1), :])
        above = jnp.where(dom == 0, 0.0, halo_in[1, pl.ds(j, 1), :])
        total = product[j] + against(lambda i: diag[i, j])
        up = pltpu.roll(against(lambda i: face[i, 0, j]), 127, 0)
        total = total + jnp.where(last, jnp.broadcast_to(below, (128, 128)), up)
        down = pltpu.roll(against(lambda i: face[i, 1, j]), 1, 0)
        total = total + jnp.where(first, jnp.broadcast_to(above, (128, 128)), down)
        total = total + jnp.where(right, 0.0, pltpu.roll(against(lambda i: face[i, 2, j]), 127, 1))
        total = total + jnp.where(left, 0.0, pltpu.roll(against(lambda i: face[i, 3, j]), 1, 1))
        product[j] = total
        return carry

    lax.fori_loop(0, 6, variable, 0)

    nodes01.wait_recv()
    owned = jnp.sum(got01[0:128], axis=0)
    for x in range(2):
        for b in range(4):
            sens[x:x + 1, b * 128:(b + 1) * 128] = owned[x * 4 + b:x * 4 + b + 1, :]
    nodes2.wait_recv()
    owned = jnp.sum(got2[0:128, 0:4, :], axis=0)
    for b in range(4):
        sens[2:3, b * 128:(b + 1) * 128] = owned[b:b + 1, :]

    for exchange in (fringes, nodes01, nodes2):
        exchange.wait_send()


def local(
    adjoint, jac_diag, jac_face, metric, node_id, fringe_cell, donor_cell, fringe_weight, donor_count
):
    vmem = pl.BlockSpec(memory_space=pltpu.VMEM)
    hbm = pl.BlockSpec(memory_space=pl.ANY)
    source = pltpu.VMEM((DEVICES, 8, 128), F32)
    target = pltpu.VMEM((DEVICES + 1, 8, 128), F32)
    product, sens = pl.pallas_call(
        kernel,
        in_specs=[vmem] * 6 + [hbm] * 3,
        out_specs=[vmem, vmem],
        out_shape=[
            jax.ShapeDtypeStruct((6, 128, 128), F32),
            jax.ShapeDtypeStruct((3, 512), F32),
        ],
        scratch_shapes=[
            pltpu.VMEM((6, 6, 128, 128), F32),
            pltpu.VMEM((6, 4, 6, 128, 128), F32),
            pltpu.VMEM((6, 3, 4, 128, 128), F32),
            pltpu.VMEM((768, 256), BF),
            pltpu.VMEM((128, 128), F32),
            pltpu.VMEM((6, 256, 256), F32),
            source, target, source, target, source, target,
            pltpu.VMEM((2, 8, 128), F32),
            pltpu.VMEM((2, 8, 128), F32),
            pltpu.SemaphoreType.DMA((3,)),
            pltpu.SemaphoreType.DMA((3,)),
            pltpu.SemaphoreType.DMA((3,)),
            pltpu.SemaphoreType.DMA((2,)),
            pltpu.SemaphoreType.DMA((2,)),
        ],
        compiler_params=pltpu.CompilerParams(
            collective_id=0, has_side_effects=True, vmem_limit_bytes=58 * 2**20
        ),
        name="adjoint_step",
    )(
        adjoint[0], fringe_cell[0], node_id[0], donor_cell[0], fringe_weight[0], donor_count,
        jac_diag[0], jac_face[0], metric[0],
    )
    return (product[None], sens)


def solution(mesh):
    in_specs = (
        P("grid", None, "dom", None),
        P("grid", None, None, "dom", None),
        P("grid", None, None, None, "dom", None),
        P("grid", None, None, None, "dom", None),
        P("grid", None, "dom", None),
        P(("dom", "grid"), None, None),
        P(("dom", "grid"), None, None),
        P(("dom", "grid"), None, None),
        P(("dom", "grid"), None),
    )
    out_specs = (P("grid", None, "dom", None), P(None, ("dom", "grid")))
    return jax.shard_map(local, mesh=mesh, in_specs=in_specs, out_specs=out_specs, check_vma=False)
```
